512 devices in a mesh: seq: 128 (over z, x_hi, y), tp: 4 (over x_lo, core).
Axes of the slice: x: 4 (x_hi: 2, x_lo: 2; x = x_hi * 2 + x_lo), y: 4, z: 16, core: 2. Of those that a mesh axis runs over, the one named last changes fastest.
Arguments:
- latent: bfloat16 [32768, 3072], P(('seq', 'tp')), may hold values from -6 to 6
- queries: bfloat16 [32768, 1536], P('seq', 'tp'), may hold values from -40 to 40
- key_vectors: bfloat16 [32768, 1536], P('seq', 'tp'), may hold values from -40 to 40
- value_vectors: bfloat16 [32768, 1536], P('seq', 'tp'), may hold values from -6 to 6
- proj_weight: bfloat16 [1536, 3072], P('tp'), may hold values from -0.15625 to 0.15625
- gate_scale: float32 [8, 3072], replicated, may hold values from -2 to 2
- text_length: int32 [8], replicated, may hold values from 64 to 128, as said below
- split_table: int32 [8, 16], replicated, may hold values from 64 to 256, as said below
Outputs:
- updated: bfloat16 [32768, 3072], P(('seq', 'tp'))
The draws below stay inside these ranges and needn't reach their ends.
Inputs may be any that keep to these rules, and one draw needn't show every extreme that they name: `text_length`: some request has exactly 128 text tokens; text tokens are the first positions of a request. `split_table`: live slots of a device are its first ones; some request has an index of its group with all 256 slots live.
All inputs are finite; a program needn't handle non-finite values.
Results may differ from the reference program's by a relative error of at most 0.0075.
Values may be sent and summed in bfloat16 or wider, within the bound.
No kernel may reach another device: no remote copies, remote signals or barrier semaphores. Data moves between devices by JAX's collectives and lax.ppermute only.
A program may use at most 64 MiB of HBM per device.

```python
import math
import jax
import jax.numpy as jnp
from jax import lax

D = 3072
HEADS = 12
HEAD_DIM = 128
TOK_DEV = 256
ITEMS = 8
TEXT_MOST = 128
GROUP = 16
SLOTS = 32768


def drawn_draw(key, first):
    drawn = jax.random.normal(jax.random.fold_in(key, first), (SLOTS, HEADS, HEAD_DIM), jnp.float32)
    return jnp.clip(drawn, -40.0, 40.0).reshape(SLOTS, HEADS * HEAD_DIM)


def draw_queries(key, part):
    return drawn_draw(key, 1).astype(jnp.bfloat16)


def draw_key_vectors(key, part):
    return drawn_draw(key, 4).astype(jnp.bfloat16)


def draw_text_length(key, part):
    drawn = jax.random.randint(jax.random.fold_in(key, 21), (ITEMS,), TEXT_MOST // 2, TEXT_MOST + 1)
    chosen = jax.random.randint(jax.random.fold_in(key, 22), (1,), 0, ITEMS)
    return jnp.where(jnp.arange(ITEMS) == chosen, TEXT_MOST, drawn).astype(jnp.int32)


def draw_split_table(key, part):
    drawn = jax.random.randint(jax.random.fold_in(key, 31), (ITEMS, GROUP), TOK_DEV // 4, TOK_DEV + 1)
    chosen = jax.random.randint(jax.random.fold_in(key, 32), (1,), 0, ITEMS * GROUP)
    flat_index = jnp.arange(ITEMS * GROUP, dtype=jnp.int32).reshape(ITEMS, GROUP)
    return jnp.where(flat_index == chosen, TOK_DEV, drawn).astype(jnp.int32)


def block_scale(own_key, extent, cuts, smallest, high):
    loudness, own = 1.0, jax.random.fold_in(own_key, 6)
    for dim, parts in cuts:
        draws = jnp.exp(jax.random.uniform(jax.random.fold_in(own, dim), (parts,), jnp.float32, smallest / len(cuts), high / len(cuts)))
        loudness = loudness * jnp.repeat(draws, extent[dim] // parts).reshape([-1 if axis == dim else 1 for axis in range(len(extent))])
    return loudness


def noise(rng, extent, spread, limit, split=(), held_as=jnp.bfloat16):
    array = spread * jax.random.normal(rng, extent, jnp.float32)
    if split:
        array = array * block_scale(rng, extent, split, -0.22, 0.18)
    return jnp.clip(array, -limit, limit).astype(held_as)


def setup_inputs(seed: int = 0) -> dict:
    arg_keys = jax.random.split(jax.random.key(seed), 9)
    latent = noise(arg_keys[0], (SLOTS, D), 1.0, 6.0, ((0, 512),))
    queries = draw_queries(jax.random.fold_in(arg_keys[8], 71), 0)
    key_vectors = draw_key_vectors(jax.random.fold_in(arg_keys[8], 71), 0)
    value_vectors = noise(arg_keys[3], (SLOTS, HEADS * HEAD_DIM), 1.0, 6.0, ((0, 128), (1, 4)))
    proj_weight = noise(arg_keys[4], (HEADS * HEAD_DIM, D), (HEADS * HEAD_DIM) ** -0.5, 0.15625, ((0, 4),))
    gate_scale = jnp.clip(jax.random.uniform(arg_keys[5], (ITEMS, D), jnp.float32, -2.0, 2.0), -2.0, 2.0)
    text_length = draw_text_length(jax.random.fold_in(arg_keys[8], 71), 0)
    split_table = draw_split_table(jax.random.fold_in(arg_keys[8], 71), 0)
    return {"latent": latent, "queries": queries, "key_vectors": key_vectors, "value_vectors": value_vectors, "proj_weight": proj_weight, "gate_scale": gate_scale, "text_length": text_length, "split_table": split_table}


def attend_head(query_head, key_head, value_head, key_live):
    scores = jnp.dot(query_head, key_head.T, preferred_element_type=jnp.float32) * (1.0 / math.sqrt(HEAD_DIM))
    scores = jnp.where(key_live[None, :], scores, -1e+30)
    top_score = lax.optimization_barrier(jnp.max(scores, axis=1, keepdims=True))
    weights = jnp.exp(scores - top_score) * key_live[None, :].astype(jnp.float32)
    weight_total = lax.optimization_barrier(jnp.sum(weights, axis=1, keepdims=True))
    summed = jnp.dot(weights.astype(jnp.bfloat16), value_head, preferred_element_type=jnp.float32)
    return (summed / weight_total).astype(jnp.bfloat16)

def reference(latent, queries, key_vectors, value_vectors, proj_weight, gate_scale, text_length, split_table):
    item_span = GROUP * TOK_DEV
    slot_index = jnp.arange(TOK_DEV, dtype=jnp.int32)
    key_live = slot_index[None, None, :] < split_table[:, :, None]
    offsets = jnp.cumsum(split_table, axis=1) - split_table
    position = offsets[:, :, None] + slot_index[None, None, :]
    image_mask = key_live & (position >= text_length[:, None, None])
    key_live = key_live.reshape(ITEMS, item_span)
    image_mask = image_mask.reshape(ITEMS, item_span)

    def heads_first(matrix):
        return matrix.reshape(item_span, HEADS, HEAD_DIM).transpose(1, 0, 2)

    def per_item(inputs):
        query_item, key_item, value_item, latent_item, live_item, image_item, gate_item = inputs

        def per_head(head_parts):
            return attend_head(head_parts[0], head_parts[1], head_parts[2], live_item)
        attended = lax.map(per_head, (heads_first(query_item), heads_first(key_item), heads_first(value_item)))
        attended = attended.transpose(1, 0, 2).reshape(item_span, HEADS * HEAD_DIM)
        projected = jnp.dot(attended, proj_weight, preferred_element_type=jnp.float32)
        residual_base = latent_item.astype(jnp.float32)
        return jnp.where(image_item[:, None], residual_base + gate_item[None, :] * projected, residual_base).astype(jnp.bfloat16)
    result = lax.map(per_item, (queries.reshape(ITEMS, item_span, HEADS * HEAD_DIM), key_vectors.reshape(ITEMS, item_span, HEADS * HEAD_DIM), value_vectors.reshape(ITEMS, item_span, HEADS * HEAD_DIM), latent.reshape(ITEMS, item_span, D), key_live, image_mask, gate_scale))
    return result.reshape(ITEMS * item_span, D)
```

```python
import math

import jax
import jax.numpy as jnp
from jax import lax
from jax.experimental import pallas as pl
from jax.experimental.pallas import tpu as pltpu
from jax.sharding import Mesh, PartitionSpec as P

HEAD_DIM = 128
GROUP = 16
LANES = 128
QMODE = "perm"
WMODE = "perm"
SCALE = math.log2(math.e) / math.sqrt(HEAD_DIM)


def place():
    z, h, y = lax.axis_index("z"), lax.axis_index("h"), lax.axis_index("y")
    return lax.axis_index("r"), z * 2 + h, y


def attend_kernel(split_ref, q0, q1, q2, q3, kv_ref, out_ref):
    request, mine, y = place()
    blocks, _, tokens, width = kv_ref.shape
    heads = width // HEAD_DIM
    keys = blocks * tokens
    quarter = tokens // 4
    slot = lax.broadcasted_iota(jnp.int32, (1, tokens), 1)
    bias = jnp.concatenate(
        [jnp.where(slot < split_ref[request, mine * 4 + b], 0.0, -1e30) for b in range(blocks)], axis=1
    )
    lane = lax.broadcasted_iota(jnp.int32, (tokens, LANES), 1)
    for d, q_ref in enumerate((q0, q1, q2, q3)):
        target = jnp.bitwise_xor(mine, d)
        stats = jnp.zeros((tokens, LANES), jnp.float32)
        for h in range(heads):
            cols = slice(h * HEAD_DIM, (h + 1) * HEAD_DIM)
            k = kv_ref[:, 0, :, cols].reshape(keys, HEAD_DIM)
            v = kv_ref[:, 1, :, cols].reshape(keys, HEAD_DIM)
            s = lax.dot_general(q_ref[:, cols], k, (((1,), (1,)), ((), ())), preferred_element_type=jnp.float32)
            s = s + bias
            top = jnp.max(s, axis=1, keepdims=True) * SCALE
            high = top.astype(jnp.bfloat16).astype(jnp.float32)
            low = (top - high + jnp.abs(top) * 2.0**-16).astype(jnp.bfloat16).astype(jnp.float32)
            p = jnp.exp2(s * SCALE - (high + low))
            total = jnp.sum(p, axis=1, keepdims=True)
            o = jnp.dot(p.astype(jnp.bfloat16), v, preferred_element_type=jnp.float32)
            ob = o.astype(jnp.bfloat16)
            for t in range(4):
                out_ref[target, t, :, cols] = ob[t * quarter:(t + 1) * quarter]
            thigh = total.astype(jnp.bfloat16).astype(jnp.float32)
            tlow = total - thigh
            for j, part in enumerate((high, low, thigh, tlow)):
                stats = jnp.where(lane == 4 * h + j, part, stats)
        sb = stats.astype(jnp.bfloat16)
        for t in range(4):
            out_ref[target, t, :, width:] = sb[t * quarter:(t + 1) * quarter]


def finish_kernel(split_ref, text_ref, part_ref, w0, w1, w2, w3, latent_ref, gate_ref, out_ref):
    request, mine, y = place()
    t_mine = lax.axis_index("l") * 2 + lax.axis_index("c")
    place_in = mine * 4 + y
    rows = latent_ref.shape[0]
    width = w0.shape[0]
    heads = width // HEAD_DIM
    acc = None
    for j, w_ref in enumerate((w0, w1, w2, w3)):
        t = jnp.bitwise_xor(t_mine, j)
        pieces = []
        stat = [part_ref[p * 4 + t, :, width:].astype(jnp.float32) for p in range(4)]
        for h in range(heads):
            cols = slice(h * HEAD_DIM, (h + 1) * HEAD_DIM)
            c = [[stat[p][:, 4 * h + i:4 * h + i + 1] for i in range(4)] for p in range(4)]
            tops = [c[p][0] + c[p][1] for p in range(4)]
            top = jnp.maximum(jnp.maximum(tops[0], tops[1]), jnp.maximum(tops[2], tops[3]))
            e = [jnp.exp2(tops[p] - top) for p in range(4)]
            total = sum(e[p] * (c[p][2] + c[p][3]) for p in range(4))
            a = sum(e[p] * part_ref[p * 4 + t, :, cols].astype(jnp.float32) for p in range(4))
            pieces.append((a / total).astype(jnp.bfloat16))
        att = jnp.concatenate(pieces, axis=1)
        d = jnp.dot(att, w_ref[...], preferred_element_type=jnp.float32)
        acc = d if acc is None else acc + d
    offset = jnp.int32(0)
    for g in range(GROUP):
        offset = offset + jnp.where(g < place_in, split_ref[request, g], 0)
    first = text_ref[request] - offset
    last = split_ref[request, place_in]
    slot = t_mine * rows + lax.broadcasted_iota(jnp.int32, (rows, 1), 0)
    image = (slot >= first) & (slot < last)
    base = latent_ref[...].astype(jnp.float32)
    gate = gate_ref[pl.ds(request, 1), :]
    out_ref[...] = jnp.where(image, base + gate * acc, base).astype(jnp.bfloat16)


def on_device(latent, queries, key_vectors, value_vectors, proj_weight, gate_scale, text_length, split_table):
    tokens, width = queries.shape
    smem = pl.BlockSpec(memory_space=pltpu.SMEM)
    vmem = pl.BlockSpec(memory_space=pltpu.VMEM)

    def swap(x, d):
        return lax.ppermute(x, ("z", "h"), [(i, i ^ d) for i in range(4)])

    if QMODE == "perm":
        qs = [queries] + [swap(queries, d) for d in (1, 2, 3)]
    stacked = jnp.stack([key_vectors, value_vectors])
    kv = lax.all_gather(stacked, "y")
    if WMODE == "perm":
        w0 = proj_weight
        route = []
        for h in range(2):
            for l in range(2):
                x = h * 2 + l
                for c in range(2):
                    sx = (x + 1) % 4 if c == 0 else (x + 3) % 4
                    route.append((sx * 2 + c, x * 2 + c))
        hop = [((sx // 4) * 4 + sx % 4, dx) for sx, dx in route]
        w2 = lax.ppermute(proj_weight, ("h", "l", "c"), hop)
        w1 = lax.ppermute(proj_weight, "c", [(0, 1), (1, 0)])
        w3 = lax.ppermute(w2, "c", [(0, 1), (1, 0)])
        ws = [w0, w1, w2, w3]
    parts = pl.pallas_call(
        attend_kernel,
        out_shape=jax.ShapeDtypeStruct((4, 4, tokens // 4, width + LANES), jnp.bfloat16),
        in_specs=[smem] + [vmem] * 5,
        out_specs=vmem,
        compiler_params=pltpu.CompilerParams(vmem_limit_bytes=40 << 20),
        name="attend",
    )(split_table, *qs, kv)
    parts = parts.reshape(16, tokens // 4, width + LANES)
    got = lax.all_to_all(parts, ("z", "h", "l", "c"), 0, 0, tiled=True)
    return pl.pallas_call(
        finish_kernel,
        out_shape=jax.ShapeDtypeStruct(latent.shape, jnp.bfloat16),
        in_specs=[smem, smem] + [vmem] * 7,
        out_specs=vmem,
        compiler_params=pltpu.CompilerParams(vmem_limit_bytes=40 << 20),
        name="finish",
    )(split_table, text_length, got, *ws, latent, gate_scale)


def solution(mesh):
    parts = Mesh(mesh.devices.reshape(-1, 2, 2, 4, 2, 2), ("r", "z", "h", "y", "l", "c"))
    seq, tp = ("r", "z", "h", "y"), ("l", "c")
    return jax.shard_map(
        on_device,
        mesh=parts,
        in_specs=(
            P(seq + tp, None), P(seq, tp), P(seq, tp), P(seq, tp), P(tp, None), P(), P(), P(),
        ),
        out_specs=P(seq + tp, None),
        check_vma=False,
    )
```

```python
import functools
import math

import jax
import jax.numpy as jnp
from jax import lax
from jax.experimental import pallas as pl
from jax.experimental.pallas import tpu as pltpu
from jax.sharding import Mesh, PartitionSpec as P

HEAD_DIM = 128
GROUP = 16
LANES = 128
SCALE = math.log2(math.e) / math.sqrt(HEAD_DIM)
SMEM = pl.BlockSpec(memory_space=pltpu.SMEM)
VMEM = pl.BlockSpec(memory_space=pltpu.VMEM)
PARAMS = pltpu.CompilerParams(vmem_limit_bytes=40 << 20)


def attend_kernel(split_ref, q0, q1, q2, q3, kv_ref, out_ref):
    request = lax.axis_index("r")
    mine_z, mine_h, side = lax.axis_index("z"), lax.axis_index("h"), lax.axis_index("l")
    mine = mine_z * 2 + mine_h
    blocks, _, tokens, width = kv_ref.shape
    heads = width // HEAD_DIM
    keys = blocks * tokens
    part = tokens // 4
    slot = lax.broadcasted_iota(jnp.int32, (1, tokens), 1)
    bias = jnp.concatenate(
        [jnp.where(slot < split_ref[request, mine * 4 + b], 0.0, -1e30) for b in range(blocks)], axis=1
    )
    lane = lax.broadcasted_iota(jnp.int32, (tokens, LANES), 1)
    for d, q_ref in enumerate((q0, q1, q2, q3)):
        z, h_block = jnp.bitwise_xor(mine_z, d // 2), jnp.bitwise_xor(mine_h, d % 2)
        places = []
        for quarter in range(4):
            core, own = quarter % 2, side == quarter // 2
            h_to = jnp.where(own | (side == core), h_block, 1 - h_block)
            start = pl.multiple_of(jnp.where(own, 0, part), part)
            places.append((z * 4 + h_to * 2 + core, pl.ds(start, part), slice(quarter * part, (quarter + 1) * part)))
        stats = jnp.zeros((tokens, LANES), jnp.float32)
        for h in range(heads):
            cols = slice(h * HEAD_DIM, (h + 1) * HEAD_DIM)
            k = kv_ref[:, 0, :, cols].reshape(keys, HEAD_DIM)
            v = kv_ref[:, 1, :, cols].reshape(keys, HEAD_DIM)
            s = lax.dot_general(q_ref[:, cols], k, (((1,), (1,)), ((), ())), preferred_element_type=jnp.float32)
            s = s + bias
            top = jnp.max(s, axis=1, keepdims=True) * SCALE
            high = top.astype(jnp.bfloat16).astype(jnp.float32)
            low = (top - high + jnp.abs(top) * 2.0**-16).astype(jnp.bfloat16).astype(jnp.float32)
            p = jnp.exp2(s * SCALE - (high + low))
            total = jnp.sum(p, axis=1, keepdims=True)
            o = jnp.dot(p.astype(jnp.bfloat16), v, preferred_element_type=jnp.float32).astype(jnp.bfloat16)
            for to, row, source in places:
                out_ref[to, row, cols] = o[source]
            total_high = total.astype(jnp.bfloat16).astype(jnp.float32)
            for j, piece in enumerate((high, low, total_high, total - total_high)):
                stats = jnp.where(lane == 4 * h + j, piece, stats)
        stats = stats.astype(jnp.bfloat16)
        for to, row, source in places:
            out_ref[to, row, width:] = stats[source]


def project_kernel(part_ref, w_mine, w_other, own_ref, give_ref):
    rows = own_ref.shape[0]
    width = w_mine.shape[0]
    heads = width // HEAD_DIM
    core = lax.axis_index("c")
    both = None
    for w_ref, head_side in ((w_mine, core), (w_other, 1 - core)):
        stat = [part_ref[2 * p + head_side, :, width:].astype(jnp.float32) for p in range(4)]
        pieces = []
        for h in range(heads):
            cols = slice(h * HEAD_DIM, (h + 1) * HEAD_DIM)
            c = [[s[:, 4 * h + i:4 * h + i + 1] for i in range(4)] for s in stat]
            tops = [x[0] + x[1] for x in c]
            top = functools.reduce(jnp.maximum, tops)
            e = [jnp.exp2(x - top) for x in tops]
            total = sum(a * (x[2] + x[3]) for a, x in zip(e, c))
            mixed = sum(a * part_ref[2 * p + head_side, :, cols].astype(jnp.float32) for p, a in enumerate(e))
            pieces.append((mixed / total).astype(jnp.bfloat16))
        product = jnp.dot(jnp.concatenate(pieces, axis=1), w_ref[...], preferred_element_type=jnp.float32)
        both = product if both is None else both + product
    own_ref[...] = both[:rows]
    give_ref[...] = both[rows:].astype(jnp.bfloat16)


def finish_kernel(split_ref, text_ref, own_ref, got_ref, latent_ref, gate_ref, out_ref):
    request = lax.axis_index("r")
    index = (lax.axis_index("z") * 2 + lax.axis_index("h")) * 4 + lax.axis_index("y")
    rows = latent_ref.shape[0]
    offset = jnp.int32(0)
    for g in range(GROUP):
        offset = offset + jnp.where(g < index, split_ref[request, g], 0)
    first = text_ref[request] - offset
    last = split_ref[request, index]
    slot = (lax.axis_index("l") * 2 + lax.axis_index("c")) * rows
    slot = slot + lax.broadcasted_iota(jnp.int32, (rows, 1), 0)
    image = (slot >= first) & (slot < last)
    base = latent_ref[...].astype(jnp.float32)
    projected = own_ref[...] + got_ref[...].astype(jnp.float32)
    gate = gate_ref[pl.ds(request, 1), :]
    out_ref[...] = jnp.where(image, base + gate * projected, base).astype(jnp.bfloat16)


def call(kernel, name, outs, specs, args):
    return pl.pallas_call(
        kernel,
        out_shape=[jax.ShapeDtypeStruct(*o) for o in outs],
        in_specs=specs,
        out_specs=[VMEM] * len(outs),
        compiler_params=PARAMS,
        name=name,
    )(*args)


def on_device(latent, queries, key_vectors, value_vectors, proj_weight, gate_scale, text_length, split_table):
    tokens, width = queries.shape
    rows, depth = latent.shape
    bf16 = jnp.bfloat16

    def swap(x, d):
        return lax.ppermute(x, ("z", "h"), [(i, i ^ d) for i in range(4)])

    stacked = jnp.broadcast_to(jnp.stack([key_vectors, value_vectors])[None], (4, 2) + key_vectors.shape)
    kv = lax.all_to_all(stacked, "y", 0, 0, tiled=True)
    q = [queries] + [swap(queries, d) for d in (1, 2, 3)]
    late_weight, _ = lax.optimization_barrier((proj_weight, q[2]))
    w_other = lax.ppermute(late_weight, "c", [(0, 1), (1, 0)])
    parts = call(
        attend_kernel, "attend", [((8, 2 * rows, width + LANES), bf16)], [SMEM] + [VMEM] * 5, (split_table, *q, kv)
    )[0]
    parts = lax.all_to_all(parts, ("z", "h", "c"), 0, 0, tiled=True)
    own, give = call(
        project_kernel, "project", [((rows, depth), jnp.float32), ((rows, depth), bf16)], [VMEM] * 3,
        (parts, proj_weight, w_other),
    )
    along = [(x * 2 + c, (x + (1 if c == 0 else 3)) % 4 * 2 + c) for x in range(4) for c in range(2)]
    got = lax.ppermute(give, ("h", "l", "c"), along)
    return call(
        finish_kernel, "finish", [((rows, depth), bf16)], [SMEM] * 2 + [VMEM] * 4,
        (split_table, text_length, own, got, latent, gate_scale),
    )[0]


def solution(mesh):
    parts = Mesh(mesh.devices.reshape(-1, 2, 2, 4, 2, 2), ("r", "z", "h", "y", "l", "c"))
    seq, tp = ("r", "z", "h", "y"), ("l", "c")
    return jax.shard_map(
        on_device,
        mesh=parts,
        in_specs=(
            P(seq + tp, None), P(seq, tp), P(seq, tp), P(seq, tp), P(tp, None), P(), P(), P(),
        ),
        out_specs=P(seq + tp, None),
        check_vma=False,
    )
```

```python
import functools
import math

import jax
import jax.numpy as jnp
from jax import lax
from jax.experimental import pallas as pl
from jax.experimental.pallas import tpu as pltpu
from jax.sharding import Mesh, PartitionSpec as P

HEAD_DIM = 128
GROUP = 16
LANES = 128
STATS = 8
SCALE = math.log2(math.e) / math.sqrt(HEAD_DIM)
SMEM = pl.BlockSpec(memory_space=pltpu.SMEM)
VMEM = pl.BlockSpec(memory_space=pltpu.VMEM)
HBM = pl.BlockSpec(memory_space=pltpu.HBM)


def attend_kernel(split_ref, q0, q1, q2, q3, kv_ref, out_ref, v_ones):
    request = lax.axis_index("r")
    mine_z, mine_h, side = lax.axis_index("z"), lax.axis_index("h"), lax.axis_index("l")
    mine = mine_z * 2 + mine_h
    blocks, _, tokens, width = kv_ref.shape
    heads = width // HEAD_DIM
    keys = blocks * tokens
    part = tokens // 4
    slot = lax.broadcasted_iota(jnp.int32, (1, tokens), 1)
    bias = jnp.concatenate(
        [jnp.where(slot < split_ref[request, mine * 4 + b], 0.0, -1e30) for b in range(blocks)], axis=1
    )
    lane = lax.broadcasted_iota(jnp.int32, (tokens, LANES), 1)
    for h in range(heads):
        v_ones[h, :, :HEAD_DIM] = kv_ref[:, 1, :, h * HEAD_DIM:(h + 1) * HEAD_DIM].reshape(keys, HEAD_DIM)
        v_ones[h, :, HEAD_DIM:] = jnp.ones((keys, LANES), jnp.bfloat16)
    for d, q_ref in enumerate((q0, q1, q2, q3)):
        z, h_block = jnp.bitwise_xor(mine_z, d // 2), jnp.bitwise_xor(mine_h, d % 2)
        places = []
        for quarter in range(4):
            core, own = quarter % 2, side == quarter // 2
            h_to = jnp.where(own | (side == core), h_block, 1 - h_block)
            start = jnp.where(own, 0, part + STATS)
            places.append((z * 4 + h_to * 2 + core, pl.multiple_of(start, 8), quarter))
        stats = jnp.zeros((tokens, LANES), jnp.float32)
        for h in range(heads):
            cols = slice(h * HEAD_DIM, (h + 1) * HEAD_DIM)
            k = kv_ref[:, 0, :, cols].reshape(keys, HEAD_DIM)
            s = lax.dot_general(q_ref[:, cols], k, (((1,), (1,)), ((), ())), preferred_element_type=jnp.float32)
            s = s + bias
            top = jnp.max(s, axis=1, keepdims=True) * SCALE
            high = top.astype(jnp.bfloat16).astype(jnp.float32)
            low = (top - high + jnp.abs(top) * 2.0**-16).astype(jnp.bfloat16).astype(jnp.float32)
            p = jnp.exp2(s * SCALE - (high + low))
            both = jnp.dot(p.astype(jnp.bfloat16), v_ones[h], preferred_element_type=jnp.float32)
            o, total = both[:, :HEAD_DIM].astype(jnp.bfloat16), both[:, HEAD_DIM:]
            for to, start, quarter in places:
                out_ref[to, pl.ds(start, part), cols] = o[quarter * part:(quarter + 1) * part]
            total_high = total.astype(jnp.bfloat16).astype(jnp.float32)
            for j, piece in enumerate((high, low, total_high, total - total_high)):
                stats = jnp.where(lane == STATS * h + j, piece, stats)
        stats = stats.T.astype(jnp.bfloat16)
        for to, start, quarter in places:
            here = slice(quarter // 2 * LANES, (quarter // 2 + 1) * LANES)
            tile = [stats[STATS * h:STATS * (h + 1), here] for h in range(heads)]
            out_ref[to, pl.ds(start + part, STATS)] = jnp.concatenate(tile, axis=1)


def project_kernel(first, part_ref, w_any, w_other, out_ref, w_mine, sems):
    count = out_ref.shape[0]
    rows = pl.ds(first, count)
    share = w_any.shape[0] // sems.shape[0]
    fetches = []
    for i in range(sems.shape[0]):
        piece = pl.ds(i * share, share)
        fetches.append(pltpu.make_async_copy(w_any.at[piece], w_mine.at[piece], sems.at[i]))
        fetches[i].start()
    width = w_other.shape[0]
    heads = width // HEAD_DIM
    core = lax.axis_index("c")
    attended = []
    for head_side in (1 - core, core):
        stat = [part_ref[2 * p + head_side, pl.ds(first + count, STATS)].astype(jnp.float32) for p in range(4)]
        stat = [s[:, h * HEAD_DIM:(h + 1) * HEAD_DIM] for s in stat for h in range(heads)]
        stat.append(jnp.zeros((LANES - STATS * len(stat), LANES), jnp.float32))
        stat = jnp.concatenate(stat, axis=0).T
        stat = jnp.where(core == 0, stat[:count], stat[LANES - count:])
        pieces = []
        for h in range(heads):
            cols = slice(h * HEAD_DIM, (h + 1) * HEAD_DIM)
            at = [STATS * (heads * p + h) for p in range(4)]
            c = [[stat[:, a + i:a + i + 1] for i in range(4)] for a in at]
            tops = [x[0] + x[1] for x in c]
            top = functools.reduce(jnp.maximum, tops)
            e = [jnp.exp2(x - top) for x in tops]
            total = sum(a * (x[2] + x[3]) for a, x in zip(e, c))
            mixed = sum(a * part_ref[2 * p + head_side, rows, cols].astype(jnp.float32) for p, a in enumerate(e))
            pieces.append((mixed / total).astype(jnp.bfloat16))
        attended.append(jnp.concatenate(pieces, axis=1))
    both = jnp.dot(attended[0], w_other[...], preferred_element_type=jnp.float32)
    for fetch in fetches:
        fetch.wait()
    both = both + jnp.dot(attended[1], w_mine[...], preferred_element_type=jnp.float32)
    out_ref[...] = both.astype(out_ref.dtype)


def finish_kernel(split_ref, text_ref, own_ref, got_ref, latent_ref, gate_ref, out_ref):
    request = lax.axis_index("r")
    index = (lax.axis_index("z") * 2 + lax.axis_index("h")) * 4 + lax.axis_index("y")
    rows = latent_ref.shape[0]
    offset = jnp.int32(0)
    for g in range(GROUP):
        offset = offset + jnp.where(g < index, split_ref[request, g], 0)
    first = text_ref[request] - offset
    last = split_ref[request, index]
    slot = (lax.axis_index("l") * 2 + lax.axis_index("c")) * rows
    slot = slot + lax.broadcasted_iota(jnp.int32, (rows, 1), 0)
    image = (slot >= first) & (slot < last)
    base = latent_ref[...].astype(jnp.float32)
    projected = own_ref[...] + got_ref[...].astype(jnp.float32)
    gate = gate_ref[pl.ds(request, 1), :]
    out_ref[...] = jnp.where(image, base + gate * projected, base).astype(jnp.bfloat16)


def call(kernel, name, outs, specs, args, scratch=(), out_spec=VMEM, room=8):
    return pl.pallas_call(
        kernel,
        out_shape=[jax.ShapeDtypeStruct(*o) for o in outs],
        in_specs=specs,
        out_specs=[out_spec] * len(outs),
        scratch_shapes=scratch,
        compiler_params=pltpu.CompilerParams(vmem_limit_bytes=room << 20),
        name=name,
    )(*args)


def in_hbm(x):
    return pltpu.with_memory_space_constraint(x, pltpu.HBM)


def on_device(latent, queries, key_vectors, value_vectors, proj_weight, gate_scale, text_length, split_table):
    tokens, width = queries.shape
    rows, depth = latent.shape
    bf16 = jnp.bfloat16

    def swap(x, d):
        return lax.ppermute(x, ("z", "h"), [(i, i ^ d) for i in range(4)])

    stacked = jnp.broadcast_to(jnp.stack([key_vectors, value_vectors])[None], (4, 2) + key_vectors.shape)
    kv = lax.all_to_all(stacked, "y", 0, 0, tiled=True)
    q = [queries] + [swap(queries, d) for d in (1, 2, 3)]
    late_weight, _ = lax.optimization_barrier((proj_weight, q[2]))
    w_other = lax.ppermute(late_weight, "c", [(0, 1), (1, 0)])
    parts = call(
        attend_kernel, "attend", [((8, 2 * (rows + STATS), width), bf16)], [SMEM] + [VMEM] * 5, (split_table, *q, kv),
        [pltpu.VMEM((width // HEAD_DIM, 4 * tokens, HEAD_DIM + LANES), bf16)], room=20,
    )[0]
    parts = lax.all_to_all(parts, ("z", "h", "c"), 0, 0, tiled=True)
    weights = (in_hbm(proj_weight), w_other)
    room = [pltpu.VMEM(proj_weight.shape, bf16), pltpu.SemaphoreType.DMA((4,))]
    give = call(
        functools.partial(project_kernel, rows + STATS), "project_given", [((rows, depth), bf16)], [VMEM, HBM, VMEM],
        (parts, *weights), room, room=12,
    )[0]
    own = call(
        functools.partial(project_kernel, 0), "project_own", [((rows, depth), jnp.float32)], [VMEM, HBM, VMEM],
        (parts, *weights), room, room=12,
    )[0]
    along = [(x * 2 + c, (x + (1 if c == 0 else 3)) % 4 * 2 + c) for x in range(4) for c in range(2)]
    got = lax.ppermute(give, ("h", "l", "c"), along)
    return call(
        finish_kernel, "finish", [((rows, depth), bf16)], [SMEM] * 2 + [VMEM] * 4,
        (split_table, text_length, own, got, latent, gate_scale),
    )[0]


def solution(mesh):
    parts = Mesh(mesh.devices.reshape(-1, 2, 2, 4, 2, 2), ("r", "z", "h", "y", "l", "c"))
    seq, tp = ("r", "z", "h", "y"), ("l", "c")
    return jax.shard_map(
        on_device,
        mesh=parts,
        in_specs=(
            P(seq + tp, None), P(seq, tp), P(seq, tp), P(seq, tp), P(tp, None), P(), P(), P(),
        ),
        out_specs=P(seq + tp, None),
        check_vma=False,
    )
```

```python
import functools
import math

import jax
import jax.numpy as jnp
from jax import lax
from jax.experimental import pallas as pl
from jax.experimental.pallas import tpu as pltpu
from jax.sharding import Mesh, PartitionSpec as P

HEAD_DIM = 128
GROUP = 16
LANES = 128
STATS = 8
SCALE = math.log2(math.e) / math.sqrt(HEAD_DIM)
SMEM = pl.BlockSpec(memory_space=pltpu.SMEM)
VMEM = pl.BlockSpec(memory_space=pltpu.VMEM)
HBM = pl.BlockSpec(memory_space=pltpu.HBM)


def attend_kernel(split_ref, q0, q1, q2, q3, kv_ref, out_ref, v_ones):
    request = lax.axis_index("r")
    column, y, first_core = lax.axis_index("z") * 2 + lax.axis_index("h"), lax.axis_index("y"), lax.axis_index("c") == 0
    mine = jnp.where(first_core, column, y)
    blocks, _, tokens, width = kv_ref.shape
    heads = width // HEAD_DIM
    keys = blocks * tokens
    part = tokens // 4
    slot = lax.broadcasted_iota(jnp.int32, (1, tokens), 1)
    bias = jnp.concatenate(
        [jnp.where(slot < split_ref[request, jnp.where(first_core, column * 4 + b, b * 4 + y)], 0.0, -1e30) for b in range(blocks)], axis=1
    )
    lane = lax.broadcasted_iota(jnp.int32, (tokens, LANES), 1)
    for h in range(heads):
        v_ones[h, :, :HEAD_DIM] = kv_ref[:, 1, :, h * HEAD_DIM:(h + 1) * HEAD_DIM].reshape(keys, HEAD_DIM)
        v_ones[h, :, HEAD_DIM:] = jnp.ones((keys, LANES), jnp.bfloat16)
    for d, q_ref in enumerate((q0, q1, q2, q3)):
        target = jnp.bitwise_xor(mine, d)
        stats = jnp.zeros((tokens, LANES), jnp.float32)
        for h in range(heads):
            cols = slice(h * HEAD_DIM, (h + 1) * HEAD_DIM)
            k = kv_ref[:, 0, :, cols].reshape(keys, HEAD_DIM)
            s = lax.dot_general(q_ref[:, cols], k, (((1,), (1,)), ((), ())), preferred_element_type=jnp.float32)
            s = s + bias
            top = jnp.max(s, axis=1, keepdims=True) * SCALE
            high = top.astype(jnp.bfloat16).astype(jnp.float32)
            low = (top - high + jnp.abs(top) * 2.0**-16).astype(jnp.bfloat16).astype(jnp.float32)
            p = jnp.exp2(s * SCALE - (high + low))
            both = jnp.dot(p.astype(jnp.bfloat16), v_ones[h], preferred_element_type=jnp.float32)
            o, total = both[:, :HEAD_DIM].astype(jnp.bfloat16), both[:, HEAD_DIM:]
            for quarter in range(4):
                start = quarter * (part + STATS)
                out_ref[target, start:start + part, cols] = o[quarter * part:(quarter + 1) * part]
            total_high = total.astype(jnp.bfloat16).astype(jnp.float32)
            for j, piece in enumerate((high, low, total_high, total - total_high)):
                stats = jnp.where(lane == STATS * h + j, piece, stats)
        stats = stats.T.astype(jnp.bfloat16)
        for quarter in range(4):
            start = quarter * (part + STATS) + part
            here = slice(quarter // 2 * LANES, (quarter // 2 + 1) * LANES)
            tile = [stats[STATS * h:STATS * (h + 1), here] for h in range(heads)]
            out_ref[target, start:start + STATS] = jnp.concatenate(tile, axis=1)


def combine_kernel(part_ref, w_any, keep_ref, give_ref, w_ref, sem):
    fetch = pltpu.make_async_copy(w_any, w_ref, sem)
    fetch.start()
    count, width = keep_ref.shape[0] // 2, keep_ref.shape[1]
    heads = width // HEAD_DIM
    side, core = lax.axis_index("l"), lax.axis_index("c")
    for ref, parity in ((keep_ref, core), (give_ref, 1 - core)):
        for chunk, pair in enumerate((side, 1 - side)):
            first = pl.multiple_of((2 * pair + parity) * (count + STATS), 8)
            stat = [part_ref[p, pl.ds(first + count, STATS)].astype(jnp.float32) for p in range(4)]
            stat = [s[:, h * HEAD_DIM:(h + 1) * HEAD_DIM] for s in stat for h in range(heads)]
            stat.append(jnp.zeros((LANES - STATS * len(stat), LANES), jnp.float32))
            stat = jnp.concatenate(stat, axis=0).T
            stat = jnp.where(parity == 0, stat[:count], stat[LANES - count:])
            for h in range(heads):
                cols = slice(h * HEAD_DIM, (h + 1) * HEAD_DIM)
                at = [STATS * (heads * p + h) for p in range(4)]
                c = [[stat[:, a + i:a + i + 1] for i in range(4)] for a in at]
                tops = [x[0] + x[1] for x in c]
                top = functools.reduce(jnp.maximum, tops)
                e = [jnp.exp2(x - top) for x in tops]
                total = sum(a * (x[2] + x[3]) for a, x in zip(e, c))
                mixed = sum(a * part_ref[p, pl.ds(first, count), cols].astype(jnp.float32) for p, a in enumerate(e))
                ref[chunk * count:(chunk + 1) * count, cols] = (mixed / total).astype(jnp.bfloat16)
    fetch.wait()


def project_kernel(first, keep_ref, got_ref, w_mine, w_other, out_ref):
    rows = slice(first, first + out_ref.shape[0])
    both = jnp.dot(keep_ref[rows], w_mine[...], preferred_element_type=jnp.float32)
    both = both + jnp.dot(got_ref[rows], w_other[...], preferred_element_type=jnp.float32)
    out_ref[...] = both.astype(out_ref.dtype)


def finish_kernel(split_ref, text_ref, own_ref, got_ref, latent_ref, gate_ref, out_ref):
    request = lax.axis_index("r")
    index = (lax.axis_index("z") * 2 + lax.axis_index("h")) * 4 + lax.axis_index("y")
    rows = latent_ref.shape[0]
    offset = jnp.int32(0)
    for g in range(GROUP):
        offset = offset + jnp.where(g < index, split_ref[request, g], 0)
    first = text_ref[request] - offset
    last = split_ref[request, index]
    slot = (lax.axis_index("l") * 2 + lax.axis_index("c")) * rows
    slot = slot + lax.broadcasted_iota(jnp.int32, (rows, 1), 0)
    image = (slot >= first) & (slot < last)
    base = latent_ref[...].astype(jnp.float32)
    projected = own_ref[...] + got_ref[...].astype(jnp.float32)
    gate = gate_ref[pl.ds(request, 1), :]
    out_ref[...] = jnp.where(image, base + gate * projected, base).astype(jnp.bfloat16)


def call(kernel, name, outs, specs, args, scratch=(), room=8):
    return pl.pallas_call(
        kernel,
        out_shape=[jax.ShapeDtypeStruct(*o) for o in outs],
        in_specs=specs,
        out_specs=[VMEM] * len(outs),
        scratch_shapes=scratch,
        compiler_params=pltpu.CompilerParams(vmem_limit_bytes=room << 20),
        name=name,
    )(*args)


def in_hbm(x):
    return pltpu.with_memory_space_constraint(x, pltpu.HBM)


def on_device(latent, queries, key_vectors, value_vectors, proj_weight, gate_scale, text_length, split_table):
    tokens, width = queries.shape
    rows, depth = latent.shape
    bf16 = jnp.bfloat16
    group = ("z", "h", "y", "c")

    def spot(column, y, core):
        return (column * 4 + y) * 2 + core

    four = range(4)
    along_y = [[[spot(i, j, core) for j in four] for i in four] for core in (0, 1)]
    across = [[[spot(j, i, core) for j in four] for i in four] for core in (0, 1)]

    def swap(x, d):
        pairs = [(spot(i, j, 0), spot(i ^ d, j, 0)) for i in four for j in four]
        pairs += [(spot(i, j, 1), spot(i, j ^ d, 1)) for i in four for j in four]
        return lax.ppermute(x, group, pairs)

    def exchange(x, groups):
        return lax.all_to_all(x, group, 0, 0, tiled=True, axis_index_groups=groups)

    is_key = lax.broadcasted_iota(jnp.int32, (4, 2) + key_vectors.shape, 1) == 0
    stacked = jnp.where(is_key, key_vectors[None, None], value_vectors[None, None])
    kv = exchange(stacked, along_y[0] + across[1])
    q = [queries] + [swap(queries, d) for d in (1, 2, 3)]
    other_core = [(0, 1), (1, 0)]
    late_weight, _ = lax.optimization_barrier((proj_weight, q[2]))
    w_other = lax.ppermute(late_weight, "c", other_core)
    parts = call(
        attend_kernel, "attend", [((4, 4 * (rows + STATS), width), bf16)], [SMEM] + [VMEM] * 5, (split_table, *q, kv),
        [pltpu.VMEM((width // HEAD_DIM, 4 * tokens, HEAD_DIM + LANES), bf16)], room=20,
    )[0]
    parts = exchange(parts, across[0] + along_y[1])
    keep, give, w_mine = call(
        combine_kernel, "combine", [((2 * rows, width), bf16)] * 2 + [(proj_weight.shape, bf16)], [VMEM, HBM],
        (parts, in_hbm(proj_weight)), [pltpu.SemaphoreType.DMA], room=12,
    )
    got = lax.ppermute(give, "c", other_core)
    operands = (keep, got, w_mine, w_other)
    give = call(
        functools.partial(project_kernel, rows), "project_given", [((rows, depth), bf16)], [VMEM] * 4, operands, room=12
    )[0]
    own = call(
        functools.partial(project_kernel, 0), "project_own", [((rows, depth), jnp.float32)], [VMEM] * 4, operands, room=12
    )[0]
    got = lax.ppermute(give, "l", [(0, 1), (1, 0)])
    return call(
        finish_kernel, "finish", [((rows, depth), bf16)], [SMEM] * 2 + [VMEM] * 4,
        (split_table, text_length, own, got, latent, gate_scale),
    )[0]


def solution(mesh):
    parts = Mesh(mesh.devices.reshape(-1, 2, 2, 4, 2, 2), ("r", "z", "h", "y", "l", "c"))
    seq, tp = ("r", "z", "h", "y"), ("l", "c")
    return jax.shard_map(
        on_device,
        mesh=parts,
        in_specs=(
            P(seq + tp, None), P(seq, tp), P(seq, tp), P(seq, tp), P(tp, None), P(), P(), P(),
        ),
        out_specs=P(seq + tp, None),
        check_vma=False,
    )
```

```python
import functools
import math

import jax
import jax.numpy as jnp
from jax import lax
from jax.experimental import pallas as pl
from jax.experimental.pallas import tpu as pltpu
from jax.sharding import Mesh, PartitionSpec as P

HEAD_DIM = 128
GROUP = 16
LANES = 128
STATS = 8
FIRST, LAST = 3, (1, 2)
SCALE = math.log2(math.e) / math.sqrt(HEAD_DIM)
SMEM = pl.BlockSpec(memory_space=pltpu.SMEM)
VMEM = pl.BlockSpec(memory_space=pltpu.VMEM)
HBM = pl.BlockSpec(memory_space=pltpu.HBM)


def attend_kernel(offsets, split_ref, q_ref, kv_a, kv_b, *refs):
    request = lax.axis_index("r")
    column, y, first_core = lax.axis_index("z") * 2 + lax.axis_index("h"), lax.axis_index("y"), lax.axis_index("c") == 0
    earlier = len(refs) == 5
    if earlier:
        sum_ref, top_ref, out_ref, k_all, v_ones = refs
    else:
        sum_ref, top_ref, k_all, v_ones = refs
    blocks, tokens, width = q_ref.shape
    heads = width // HEAD_DIM
    part = tokens // 4
    slot = lax.broadcasted_iota(jnp.int32, (1, tokens), 1)
    owners = [jnp.where(first_core, column * 4 + (y ^ b), (column ^ b) * 4 + y) for b in offsets]
    bias = jnp.concatenate([jnp.where(slot < split_ref[request, i], 0.0, -1e30) for i in owners], axis=1)
    lane = lax.broadcasted_iota(jnp.int32, (tokens, LANES), 1)
    for b, kv_ref in enumerate((kv_a, kv_b)):
        rows = slice(b * tokens, (b + 1) * tokens)
        k_all[rows] = kv_ref[0]
        for h in range(heads):
            v_ones[h, rows, :HEAD_DIM] = kv_ref[1, :, h * HEAD_DIM:(h + 1) * HEAD_DIM]
            v_ones[h, rows, HEAD_DIM:] = jnp.ones((tokens, LANES), jnp.bfloat16)
    for target in range(blocks):
        stats = jnp.zeros((tokens, LANES), jnp.float32)
        for h in range(heads):
            cols = slice(h * HEAD_DIM, (h + 1) * HEAD_DIM)
            s = lax.dot_general(
                q_ref[target, :, cols], k_all[:, cols], (((1,), (1,)), ((), ())), preferred_element_type=jnp.float32
            )
            s = s + bias
            top = jnp.broadcast_to(jnp.max(s, axis=1, keepdims=True) * SCALE, (tokens, LANES))
            if earlier:
                before = top_ref[target, h]
                top = jnp.maximum(top, before)
            high = top.astype(jnp.bfloat16).astype(jnp.float32)
            low = (top - high + jnp.abs(top) * 2.0**-16).astype(jnp.bfloat16).astype(jnp.float32)
            p = jnp.exp2(s * SCALE - jnp.tile(high + low, (1, s.shape[1] // LANES)))
            both = jnp.dot(p.astype(jnp.bfloat16), v_ones[h], preferred_element_type=jnp.float32)
            if not earlier:
                sum_ref[target, h] = both
                top_ref[target, h] = high + low
                continue
            shrink = jnp.exp2(before - (high + low))
            o = (both[:, :HEAD_DIM] + shrink * sum_ref[target, h, :, :HEAD_DIM]).astype(jnp.bfloat16)
            total = both[:, HEAD_DIM:] + shrink * sum_ref[target, h, :, HEAD_DIM:]
            for quarter in range(4):
                start = quarter * (part + STATS)
                out_ref[target, start:start + part, cols] = o[quarter * part:(quarter + 1) * part]
            total_high = total.astype(jnp.bfloat16).astype(jnp.float32)
            for j, piece in enumerate((high, low, total_high, total - total_high)):
                stats = jnp.where(lane == STATS * h + j, piece, stats)
        if not earlier:
            continue
        stats = stats.T.astype(jnp.bfloat16)
        for quarter in range(4):
            start = quarter * (part + STATS) + part
            here = slice(quarter // 2 * LANES, (quarter // 2 + 1) * LANES)
            tile = [stats[STATS * h:STATS * (h + 1), here] for h in range(heads)]
            out_ref[target, start:start + STATS] = jnp.concatenate(tile, axis=1)


def combine_kernel(part_ref, w_any, keep_ref, give_ref, w_ref, sem):
    fetch = pltpu.make_async_copy(w_any, w_ref, sem)
    fetch.start()
    count, width = keep_ref.shape[0] // 2, keep_ref.shape[1]
    heads = width // HEAD_DIM
    side, core = lax.axis_index("l"), lax.axis_index("c")
    for ref, parity in ((keep_ref, core), (give_ref, 1 - core)):
        for chunk, pair in enumerate((side, 1 - side)):
            first = pl.multiple_of((2 * pair + parity) * (count + STATS), 8)
            stat = [part_ref[p, pl.ds(first + count, STATS)].astype(jnp.float32) for p in range(4)]
            stat = [s[:, h * HEAD_DIM:(h + 1) * HEAD_DIM] for s in stat for h in range(heads)]
            stat.append(jnp.zeros((LANES - STATS * len(stat), LANES), jnp.float32))
            stat = jnp.concatenate(stat, axis=0).T
            stat = jnp.where(parity == 0, stat[:count], stat[LANES - count:])
            for h in range(heads):
                cols = slice(h * HEAD_DIM, (h + 1) * HEAD_DIM)
                at = [STATS * (heads * p + h) for p in range(4)]
                c = [[stat[:, a + i:a + i + 1] for i in range(4)] for a in at]
                tops = [x[0] + x[1] for x in c]
                top = functools.reduce(jnp.maximum, tops)
                e = [jnp.exp2(x - top) for x in tops]
                total = sum(a * (x[2] + x[3]) for a, x in zip(e, c))
                mixed = sum(a * part_ref[p, pl.ds(first, count), cols].astype(jnp.float32) for p, a in enumerate(e))
                ref[chunk * count:(chunk + 1) * count, cols] = (mixed / total).astype(jnp.bfloat16)
    fetch.wait()


def project_kernel(first, keep_ref, got_ref, w_mine, w_other, out_ref):
    rows = slice(first, first + out_ref.shape[0])
    both = jnp.dot(keep_ref[rows], w_mine[...], preferred_element_type=jnp.float32)
    both = both + jnp.dot(got_ref[rows], w_other[...], preferred_element_type=jnp.float32)
    out_ref[...] = both.astype(out_ref.dtype)


def finish_kernel(split_ref, text_ref, own_ref, got_ref, latent_ref, gate_ref, out_ref):
    request = lax.axis_index("r")
    index = (lax.axis_index("z") * 2 + lax.axis_index("h")) * 4 + lax.axis_index("y")
    rows = latent_ref.shape[0]
    offset = jnp.int32(0)
    for g in range(GROUP):
        offset = offset + jnp.where(g < index, split_ref[request, g], 0)
    first = text_ref[request] - offset
    last = split_ref[request, index]
    slot = (lax.axis_index("l") * 2 + lax.axis_index("c")) * rows
    slot = slot + lax.broadcasted_iota(jnp.int32, (rows, 1), 0)
    image = (slot >= first) & (slot < last)
    base = latent_ref[...].astype(jnp.float32)
    projected = own_ref[...] + got_ref[...].astype(jnp.float32)
    gate = gate_ref[pl.ds(request, 1), :]
    out_ref[...] = jnp.where(image, base + gate * projected, base).astype(jnp.bfloat16)


def call(kernel, name, outs, specs, args, scratch=(), room=8):
    return pl.pallas_call(
        kernel,
        out_shape=[jax.ShapeDtypeStruct(*o) for o in outs],
        in_specs=specs,
        out_specs=[VMEM] * len(outs),
        scratch_shapes=scratch,
        compiler_params=pltpu.CompilerParams(vmem_limit_bytes=room << 20),
        name=name,
    )(*args)


def in_hbm(x):
    return pltpu.with_memory_space_constraint(x, pltpu.HBM)


def on_device(latent, queries, key_vectors, value_vectors, proj_weight, gate_scale, text_length, split_table):
    tokens, width = queries.shape
    rows, depth = latent.shape
    bf16 = jnp.bfloat16
    group = ("z", "h", "y", "c")

    def spot(column, y, core):
        return (column * 4 + y) * 2 + core

    four = range(4)
    along_y = [[[spot(i, j, core) for j in four] for i in four] for core in (0, 1)]
    across = [[[spot(j, i, core) for j in four] for i in four] for core in (0, 1)]

    def swap(x, d):
        pairs = [(spot(i, j, 0), spot(i, j ^ d, 0)) for i in four for j in four]
        pairs += [(spot(i, j, 1), spot(i ^ d, j, 1)) for i in four for j in four]
        return lax.ppermute(x, group, pairs)

    def exchange(x, groups):
        return lax.all_to_all(x, group, 0, 0, tiled=True, axis_index_groups=groups)

    stacked = jnp.stack([key_vectors, value_vectors])
    kv = [stacked] + [swap(stacked, d) for d in (1, 2, 3)]
    q = exchange(jnp.broadcast_to(queries[None], (4,) + queries.shape), across[0] + along_y[1])
    other_core = [(0, 1), (1, 0)]
    late_weight, _ = lax.optimization_barrier((proj_weight, kv[LAST[0]]))
    w_other = lax.ppermute(late_weight, "c", other_core)
    held = [pltpu.VMEM((2 * tokens, width), bf16)]
    held.append(pltpu.VMEM((width // HEAD_DIM, 2 * tokens, HEAD_DIM + LANES), bf16))
    state = call(
        functools.partial(attend_kernel, (0, FIRST)), "attend_early",
        [((4, width // HEAD_DIM, tokens, n), jnp.float32) for n in (HEAD_DIM + LANES, LANES)], [SMEM] + [VMEM] * 3,
        (split_table, q, kv[0], kv[FIRST]), held, room=20,
    )
    parts = call(
        functools.partial(attend_kernel, LAST), "attend_late", [((4, 4 * (rows + STATS), width), bf16)],
        [SMEM] + [VMEM] * 5, (split_table, q, kv[LAST[0]], kv[LAST[1]], *state), held, room=20,
    )[0]
    parts = exchange(parts, across[0] + along_y[1])
    keep, give, w_mine = call(
        combine_kernel, "combine", [((2 * rows, width), bf16)] * 2 + [(proj_weight.shape, bf16)], [VMEM, HBM],
        (parts, in_hbm(proj_weight)), [pltpu.SemaphoreType.DMA], room=12,
    )
    got = lax.ppermute(give, "c", other_core)
    operands = (keep, got, w_mine, w_other)
    give = call(
        functools.partial(project_kernel, rows), "project_given", [((rows, depth), bf16)], [VMEM] * 4, operands, room=12
    )[0]
    own = call(
        functools.partial(project_kernel, 0), "project_own", [((rows, depth), jnp.float32)], [VMEM] * 4, operands, room=12
    )[0]
    got = lax.ppermute(give, "l", [(0, 1), (1, 0)])
    return call(
        finish_kernel, "finish", [((rows, depth), bf16)], [SMEM] * 2 + [VMEM] * 4,
        (split_table, text_length, own, got, latent, gate_scale),
    )[0]


def solution(mesh):
    parts = Mesh(mesh.devices.reshape(-1, 2, 2, 4, 2, 2), ("r", "z", "h", "y", "l", "c"))
    seq, tp = ("r", "z", "h", "y"), ("l", "c")
    return jax.shard_map(
        on_device,
        mesh=parts,
        in_specs=(
            P(seq + tp, None), P(seq, tp), P(seq, tp), P(seq, tp), P(tp, None), P(), P(), P(),
        ),
        out_specs=P(seq + tp, None),
        check_vma=False,
    )
```

```python
import functools
import math

import jax
import jax.numpy as jnp
from jax import lax
from jax.experimental import pallas as pl
from jax.experimental.pallas import tpu as pltpu
from jax.sharding import Mesh, PartitionSpec as P

HEAD_DIM = 128
GROUP = 16
LANES = 128
STATS = 8
SCALE = math.log2(math.e) / math.sqrt(HEAD_DIM)
SMEM = pl.BlockSpec(memory_space=pltpu.SMEM)
VMEM = pl.BlockSpec(memory_space=pltpu.VMEM)
HBM = pl.BlockSpec(memory_space=pltpu.HBM)


def attend_kernel(split_ref, q0, q1, q2, q3, kv_ref, out_ref, v_ones):
    request = lax.axis_index("r")
    mine_z, mine_h, side = lax.axis_index("z"), lax.axis_index("h"), lax.axis_index("l")
    mine = mine_z * 2 + mine_h
    blocks, _, tokens, width = kv_ref.shape
    heads = width // HEAD_DIM
    keys = blocks * tokens
    part = tokens // 4
    slot = lax.broadcasted_iota(jnp.int32, (1, tokens), 1)
    bias = jnp.concatenate(
        [jnp.where(slot < split_ref[request, mine * 4 + b], 0.0, -1e30) for b in range(blocks)], axis=1
    )
    lane = lax.broadcasted_iota(jnp.int32, (tokens, LANES), 1)
    for h in range(heads):
        v_ones[h, :, :HEAD_DIM] = kv_ref[:, 1, :, h * HEAD_DIM:(h + 1) * HEAD_DIM].reshape(keys, HEAD_DIM)
        v_ones[h, :, HEAD_DIM:] = jnp.ones((keys, LANES), jnp.bfloat16)
    for d, q_ref in enumerate((q0, q1, q2, q3)):
        z, h_block = jnp.bitwise_xor(mine_z, d // 2), jnp.bitwise_xor(mine_h, d % 2)
        places = []
        for quarter in range(4):
            core, own = quarter % 2, side == quarter // 2
            h_to = jnp.where(own | (side == core), h_block, 1 - h_block)
            start = jnp.where(own, 0, part + STATS)
            places.append((z * 4 + h_to * 2 + core, pl.multiple_of(start, 8), quarter))
        stats = jnp.zeros((tokens, LANES), jnp.float32)
        for h in range(heads):
            cols = slice(h * HEAD_DIM, (h + 1) * HEAD_DIM)
            k = kv_ref[:, 0, :, cols].reshape(keys, HEAD_DIM)
            s = lax.dot_general(q_ref[:, cols], k, (((1,), (1,)), ((), ())), preferred_element_type=jnp.float32)
            s = s + bias
            top = jnp.broadcast_to(jnp.max(s, axis=1, keepdims=True) * SCALE, (tokens, LANES))
            high = top.astype(jnp.bfloat16).astype(jnp.float32)
            low = (top - high + jnp.abs(top) * 2.0**-16).astype(jnp.bfloat16).astype(jnp.float32)
            p = jnp.exp2(s * SCALE - jnp.tile(high + low, (1, keys // LANES)))
            both = jnp.dot(p.astype(jnp.bfloat16), v_ones[h], preferred_element_type=jnp.float32)
            o, total = both[:, :HEAD_DIM].astype(jnp.bfloat16), both[:, HEAD_DIM:]
            for to, start, quarter in places:
                out_ref[to, pl.ds(start, part), cols] = o[quarter * part:(quarter + 1) * part]
            total_high = total.astype(jnp.bfloat16).astype(jnp.float32)
            for j, piece in enumerate((high, low, total_high, total - total_high)):
                stats = jnp.where(lane == STATS * h + j, piece, stats)
        stats = stats.T.astype(jnp.bfloat16)
        for to, start, quarter in places:
            here = slice(quarter // 2 * LANES, (quarter // 2 + 1) * LANES)
            tile = [stats[STATS * h:STATS * (h + 1), here] for h in range(heads)]
            out_ref[to, pl.ds(start + part, STATS)] = jnp.concatenate(tile, axis=1)


def project_kernel(first, part_ref, w_any, w_other, out_ref, w_mine, sems):
    count = out_ref.shape[0]
    rows = pl.ds(first, count)
    share = w_any.shape[1] // sems.shape[0]
    fetches = []
    for i in range(sems.shape[0]):
        piece = (slice(None), pl.ds(i * share, share))
        fetches.append(pltpu.make_async_copy(w_any.at[piece], w_mine.at[piece], sems.at[i]))
        fetches[i].start()
    width = w_other.shape[0]
    heads = width // HEAD_DIM
    core = lax.axis_index("c")
    attended = []
    for head_side in (1 - core, core):
        stat = [part_ref[2 * p + head_side, pl.ds(first + count, STATS)].astype(jnp.float32) for p in range(4)]
        stat = [s[:, h * HEAD_DIM:(h + 1) * HEAD_DIM] for s in stat for h in range(heads)]
        stat.append(jnp.zeros((LANES - STATS * len(stat), LANES), jnp.float32))
        stat = jnp.concatenate(stat, axis=0).T
        stat = jnp.where(core == 0, stat[:count], stat[LANES - count:])
        pieces = []
        for h in range(heads):
            cols = slice(h * HEAD_DIM, (h + 1) * HEAD_DIM)
            at = [STATS * (heads * p + h) for p in range(4)]
            c = [[stat[:, a + i:a + i + 1] for i in range(4)] for a in at]
            tops = [x[0] + x[1] for x in c]
            top = functools.reduce(jnp.maximum, tops)
            e = [jnp.exp2(x - top) for x in tops]
            total = sum(a * (x[2] + x[3]) for a, x in zip(e, c))
            mixed = sum(a * part_ref[2 * p + head_side, rows, cols].astype(jnp.float32) for p, a in enumerate(e))
            pieces.append((mixed / total).astype(jnp.bfloat16))
        attended.append(jnp.concatenate(pieces, axis=1))
    for i, fetch in enumerate(fetches):
        cols = slice(i * share, (i + 1) * share)
        both = jnp.dot(attended[0], w_other[:, cols], preferred_element_type=jnp.float32)
        fetch.wait()
        both = both + jnp.dot(attended[1], w_mine[:, cols], preferred_element_type=jnp.float32)
        out_ref[:, cols] = both.astype(out_ref.dtype)


def finish_kernel(split_ref, text_ref, own_ref, got_ref, latent_ref, gate_ref, out_ref):
    request = lax.axis_index("r")
    index = (lax.axis_index("z") * 2 + lax.axis_index("h")) * 4 + lax.axis_index("y")
    rows = latent_ref.shape[0]
    offset = jnp.int32(0)
    for g in range(GROUP):
        offset = offset + jnp.where(g < index, split_ref[request, g], 0)
    first = text_ref[request] - offset
    last = split_ref[request, index]
    slot = (lax.axis_index("l") * 2 + lax.axis_index("c")) * rows
    slot = slot + lax.broadcasted_iota(jnp.int32, (rows, 1), 0)
    image = (slot >= first) & (slot < last)
    base = latent_ref[...].astype(jnp.float32)
    projected = own_ref[...] + got_ref[...].astype(jnp.float32)
    gate = gate_ref[pl.ds(request, 1), :]
    out_ref[...] = jnp.where(image, base + gate * projected, base).astype(jnp.bfloat16)


def call(kernel, name, outs, specs, args, scratch=(), out_spec=VMEM, room=8):
    return pl.pallas_call(
        kernel,
        out_shape=[jax.ShapeDtypeStruct(*o) for o in outs],
        in_specs=specs,
        out_specs=[out_spec] * len(outs),
        scratch_shapes=scratch,
        compiler_params=pltpu.CompilerParams(vmem_limit_bytes=room << 20),
        name=name,
    )(*args)


def in_hbm(x):
    return pltpu.with_memory_space_constraint(x, pltpu.HBM)


def on_device(latent, queries, key_vectors, value_vectors, proj_weight, gate_scale, text_length, split_table):
    tokens, width = queries.shape
    rows, depth = latent.shape
    bf16 = jnp.bfloat16

    def swap(x, d):
        return lax.ppermute(x, ("z", "h"), [(i, i ^ d) for i in range(4)])

    stacked = jnp.broadcast_to(jnp.stack([key_vectors, value_vectors])[None], (4, 2) + key_vectors.shape)
    kv = lax.all_to_all(stacked, "y", 0, 0, tiled=True)
    q = [queries] + [swap(queries, d) for d in (1, 2, 3)]
    late_weight, _ = lax.optimization_barrier((proj_weight, q[2]))
    w_other = lax.ppermute(late_weight, "c", [(0, 1), (1, 0)])
    parts = call(
        attend_kernel, "attend", [((8, 2 * (rows + STATS), width), bf16)], [SMEM] + [VMEM] * 5, (split_table, *q, kv),
        [pltpu.VMEM((width // HEAD_DIM, 4 * tokens, HEAD_DIM + LANES), bf16)], room=20,
    )[0]
    parts = lax.all_to_all(parts, ("z", "h", "c"), 0, 0, tiled=True)
    weights = (in_hbm(proj_weight), w_other)
    room = [pltpu.VMEM(proj_weight.shape, bf16), pltpu.SemaphoreType.DMA((4,))]
    give = call(
        functools.partial(project_kernel, rows + STATS), "project_given", [((rows, depth), bf16)], [VMEM, HBM, VMEM],
        (parts, *weights), room, room=12,
    )[0]
    own = call(
        functools.partial(project_kernel, 0), "project_own", [((rows, depth), jnp.float32)], [VMEM, HBM, VMEM],
        (parts, *weights), room, room=12,
    )[0]
    along = [(x * 2 + c, (x + (1 if c == 0 else 3)) % 4 * 2 + c) for x in range(4) for c in range(2)]
    got = lax.ppermute(give, ("h", "l", "c"), along)
    return call(
        finish_kernel, "finish", [((rows, depth), bf16)], [SMEM] * 2 + [VMEM] * 4,
        (split_table, text_length, own, got, latent, gate_scale),
    )[0]


def solution(mesh):
    parts = Mesh(mesh.devices.reshape(-1, 2, 2, 4, 2, 2), ("r", "z", "h", "y", "l", "c"))
    seq, tp = ("r", "z", "h", "y"), ("l", "c")
    return jax.shard_map(
        on_device,
        mesh=parts,
        in_specs=(
            P(seq + tp, None), P(seq, tp), P(seq, tp), P(seq, tp), P(tp, None), P(), P(), P(),
        ),
        out_specs=P(seq + tp, None),
        check_vma=False,
    )
```
